32 devices in a mesh: row: 4 (over z), col: 8 (over y, x, core).
Axes of the slice: x: 2, y: 2, z: 4, core: 2. Of those that a mesh axis runs over, the one named last changes fastest.
Arguments:
- ainv: float32 [4, 512, 2, 1024], P(None, 'row', None, 'col'), may hold values from -6 to 6
- lhat_first: float32 [4, 512, 512], P(None, ('row', 'col')), may hold values from -0.15625 to 0.15625
- lhat_second: float32 [4, 512, 512], P(None, ('row', 'col')), may hold values from -0.1875 to 0.1875
- second_on_first: float32 [512, 512], replicated, may hold values from -0.25 to 0.25
- dinv_first: float32 [512, 512], P(None, 'col'), may hold values from -6 to 6
- dinv_second: float32 [512, 512], P(None, 'col'), may hold values from -6 to 6
- anc_first: int32 [12], replicated, may hold values from 0 to 15, as said below
- anc_second: int32 [8], replicated, may hold values from 0 to 15, as said below
Outputs:
- cross_first: float32 [4, 512, 512], P(None, 'row', 'col')
- diag_first: float32 [512, 512], P(None, 'col')
- cross_second: float32 [4, 512, 512], P(None, 'row', 'col')
- link_second: float32 [512, 512], P(None, 'col')
- diag_second: float32 [512, 512], P(None, 'col')
The draws below stay inside these ranges and needn't reach their ends.
Inputs may be any that keep to these rules, and one draw needn't show every extreme that they name: `anc_first`: 12 different tile numbers in increasing order. `anc_second`: 8 different tile numbers in increasing order, each also listed in anc_first.
All inputs are finite; a program needn't handle non-finite values.
Results may differ from the reference program's by a relative error of at most 0.000088.
Values sent between devices are 32-bit elements; how exact they have to be, the bound alone decides.
No kernel may reach another device: no remote copies, remote signals or barrier semaphores. Data moves between devices by JAX's collectives and lax.ppermute only.
A program may use at most 64 MiB of HBM per device.

```python
import jax
import jax.numpy as jnp
from jax import lax

KW = 512
TILE = 128
STRIPS = 2
NT = 16
NL1 = 12
NL2 = 8
N_ROW = 4
N_COL = 8


def ancestor_sets(key):
    order = jax.random.permutation(jax.random.fold_in(key, 7), NT)
    first = jnp.sort(order[:NL1]).astype(jnp.int32)
    pick = jax.random.permutation(jax.random.fold_in(key, 11), NL1)
    second = jnp.sort(first[pick[:NL2]]).astype(jnp.int32)
    return (first, second)


def draw_anc_first(key, part):
    return ancestor_sets(key)[0]


def draw_anc_second(key, part):
    return ancestor_sets(key)[1]


def shard_levels(key, dims, shards, smallest, top_value):
    def one(axis_at, shards_of):
        steps = jax.random.uniform(jax.random.fold_in(jax.random.fold_in(key, 6), axis_at), (shards_of,), jnp.float32, smallest / len(shards), top_value / len(shards))
        return jnp.repeat(jnp.exp(steps), dims[axis_at] // shards_of).reshape((-1,) + (1,) * (len(dims) - axis_at - 1))

    factor_of = one(*shards[0])
    for cut in shards[1:]:
        factor_of = factor_of * one(*cut)
    return factor_of


def centred(rng, dims, scale, limit, cuts=(), kind=jnp.bfloat16):
    result = jax.random.normal(rng, dims, jnp.float32) * scale
    if len(cuts) > 0:
        result = shard_levels(rng, dims, cuts, -0.22, 0.18) * result
    return jnp.clip(result, min=-limit, max=limit).astype(kind)


def setup_inputs(seed: int = 0) -> dict:
    keys = jax.random.split(jax.random.key(seed), 9)
    ainv = centred(keys[0], (NT // N_ROW, N_ROW * TILE, STRIPS, N_COL * TILE), 1.0, 6.0, ((1, 4), (3, 8)), jnp.float32)
    lhat_first = centred(keys[1], (NT // N_ROW, N_ROW * TILE, KW), (NL1 * TILE) ** -0.5, 0.15625, ((1, 32),), jnp.float32)
    lhat_second = centred(keys[2], (NT // N_ROW, N_ROW * TILE, KW), (NL2 * TILE) ** -0.5, 0.1875, ((1, 32),), jnp.float32)
    second_on_first = centred(keys[3], (KW, KW), KW ** -0.5, 0.25, (), jnp.float32)
    dinv_first = centred(keys[4], (KW, KW), 1.0, 6.0, ((1, 8),), jnp.float32)
    dinv_second = centred(keys[5], (KW, KW), 1.0, 6.0, ((1, 8),), jnp.float32)
    anc_first = draw_anc_first(jax.random.fold_in(keys[8], 71), 0)
    anc_second = draw_anc_second(jax.random.fold_in(keys[8], 71), 0)
    return {"ainv": ainv, "lhat_first": lhat_first, "lhat_second": lhat_second, "second_on_first": second_on_first, "dinv_first": dinv_first, "dinv_second": dinv_second, "anc_first": anc_first, "anc_second": anc_second}


def product(left, right):
    return jnp.dot(left, right, precision=lax.Precision.HIGHEST, preferred_element_type=jnp.float32)


def reference(ainv, lhat_first, lhat_second, second_on_first, dinv_first, dinv_second, anc_first, anc_second):
    inverse = ainv.reshape(NT * TILE, NT * TILE)
    tiles = jnp.arange(NT, dtype=jnp.int32)

    def row_keep(listing):
        listed = jnp.any(tiles[:, None] == listing[None, :].astype(jnp.int32), axis=1)
        return jnp.repeat(listed.astype(jnp.float32), TILE)[:, None]

    keep_first = row_keep(anc_first)
    keep_second = row_keep(anc_second)
    left_first = lhat_first.reshape(NT * TILE, KW) * keep_first
    left_second = lhat_second.reshape(NT * TILE, KW) * keep_second
    cross_first = -keep_first * product(inverse, left_first)
    diag_first = dinv_first - product(left_first.T, cross_first)
    cross_second = -keep_second * (product(inverse, left_second) + product(cross_first, second_on_first))
    link_second = -(product(cross_first.T, left_second) + product(diag_first.T, second_on_first))
    diag_second = dinv_second - (product(left_second.T, cross_second) + product(second_on_first.T, link_second))
    shape_out = (NT // N_ROW, N_ROW * TILE, KW)
    return cross_first.reshape(shape_out), diag_first, cross_second.reshape(shape_out), link_second, diag_second
```

```python
import jax
import jax.numpy as jnp
from jax import lax
from jax.sharding import PartitionSpec as P


def dot(left, right, dims):
    return lax.dot_general(
        left,
        right,
        (dims, ((), ())),
        precision=lax.Precision.HIGHEST,
        preferred_element_type=jnp.float32,
    )


def xor_swap(array, axis, mask):
    count = lax.axis_size(axis)
    return lax.ppermute(array, axis, [(i, i ^ mask) for i in range(count)])


def pick(array, index, axis=0):
    return lax.dynamic_index_in_dim(array, index, axis, keepdims=False)


def body(ainv, lhat_first, lhat_second, second_on_first, dinv_first, dinv_second, anc_first, anc_second):
    rows = lax.axis_size("row")
    cols = lax.axis_size("col")
    row = lax.axis_index("row")
    col = lax.axis_index("col")
    ratio = cols // rows
    group, member = col // rows, col % rows
    local, tile, strips, _ = ainv.shape
    piece, width = lhat_first.shape[1], lhat_first.shape[2]
    share = dinv_first.shape[1]

    row_tiles = jnp.arange(local, dtype=jnp.int32) * rows + row

    def tile_keep(listing):
        listed = jnp.any(row_tiles[:, None] == listing[None, :], axis=1)
        return listed.astype(jnp.float32)

    keep_first, keep_second = tile_keep(anc_first), tile_keep(anc_second)
    first = lhat_first * keep_first[:, None, None]
    second = lhat_second * keep_second[:, None, None] - dot(
        first.reshape(local * piece, width), second_on_first, ((1,), (0,))
    ).reshape(local, piece, width)

    def gather_rows(block):
        own = [(m, xor_swap(block, "col", m) if m else block) for m in range(0, cols, 2)]
        other = xor_swap(jnp.stack([b for _, b in own]), "col", 1)
        blocks = own + [(m + 1, other[i]) for i, (m, _) in enumerate(own)]
        full = jnp.zeros((local, tile, width), jnp.float32)
        for m, b in blocks:
            full = lax.dynamic_update_slice(full, b, (0, (col ^ m) * piece, 0))
        return full

    def spread(full):
        mine = pick(full.reshape(strips, ratio, tile, width), group, 1)
        mine = pick(mine.reshape(strips, tile, ratio, rows, share), member, 3)
        mine = mine.transpose(2, 3, 0, 1).reshape(1, ratio * share, strips * tile)
        out = jnp.zeros((rows, ratio * share, strips * tile), jnp.float32)
        for m in range(rows):
            part = xor_swap(mine, "row", m) if m else mine
            out = lax.dynamic_update_slice(out, part, (row ^ m, 0, 0))
        return out

    square = ainv.reshape(1, local * tile, strips * tile)
    order, held, bit = [0], square, rows // 2
    while bit:
        held = jnp.concatenate([held, xor_swap(held, "col", bit)])
        order = order + [m ^ bit for m in order]
        bit //= 2
    panel = jnp.zeros_like(held)
    for i, m in enumerate(order):
        panel = lax.dynamic_update_slice(panel, held[i : i + 1], (member ^ m, 0, 0))

    def multiply(blocks):
        part = dot(blocks, panel, ((0, 2), (0, 2))).reshape(ratio, share, local * tile)
        total = pick(part, group)
        for m in range(1, ratio):
            total = total + xor_swap(pick(part, group ^ m), "col", m * rows)
        return total

    def result(total, keep):
        out = total.T.reshape(local, tile, share)
        return -keep[:, None, None] * out

    full_first = gather_rows(first)
    full_second = gather_rows(second)
    u = multiply(spread(full_first))
    v = multiply(spread(full_second))
    flat_first = full_first.reshape(local * tile, width)
    flat_second = full_second.reshape(local * tile, width)
    x = dot(u, flat_first, ((1,), (0,)))
    own = dot(dinv_first, second_on_first, ((0,), (0,)))
    link_rows = dot(u, flat_second, ((1,), (0,))) - jnp.where(row == 0, own, 0.0)
    link = link_rows.reshape(share, cols, share).transpose(1, 0, 2)
    link = lax.all_to_all(link, "col", 0, 0, tiled=True)
    link = link.transpose(2, 0, 1).reshape(share, width)
    z = dot(v, flat_second, ((1,), (0,))) + dot(
        dot(v, flat_first, ((1,), (0,))) - link, second_on_first, ((1,), (0,))
    )
    stacked = jnp.concatenate([x, link, z])
    chunks = stacked.reshape(3 * share, rows, width // rows).transpose(1, 0, 2)
    total = pick(chunks, row)
    for m in range(1, rows):
        total = total + xor_swap(pick(chunks, row ^ m), "row", m)
    out = jnp.zeros_like(stacked)
    for m in range(rows):
        part = xor_swap(total, "row", m) if m else total
        out = lax.dynamic_update_slice(out, part, (0, (row ^ m) * (width // rows)))
    x, link, z = (out[i * share : (i + 1) * share].T for i in range(3))
    return result(u, keep_first), dinv_first + x, result(v, keep_second), link, dinv_second + z


def solution(mesh):
    return jax.shard_map(
        body,
        mesh=mesh,
        in_specs=(
            P(None, "row", None, "col"),
            P(None, ("row", "col"), None),
            P(None, ("row", "col"), None),
            P(),
            P(None, "col"),
            P(None, "col"),
            P(),
            P(),
        ),
        out_specs=(
            P(None, "row", "col"),
            P(None, "col"),
            P(None, "row", "col"),
            P(None, "col"),
            P(None, "col"),
        ),
        check_vma=False,
    )
```
